32 devices in a mesh: sub: 8 (over y, x, core), fac: 4 (over z).
Axes of the slice: x: 2, y: 2, z: 4, core: 2. Of those that a mesh axis runs over, the one named last changes fastest.
Arguments:
- subgrids: bfloat16 [2, 64, 512, 512], P(None, 'sub', 'fac'), may hold values from -6 to 6
- sub_offsets: int32 [64, 2], replicated, may hold values from 0 to 127, as said below
- coverage: int32 [64], replicated, may hold values from 0 to 1, as said below
- facet_offsets: int32 [2, 4], replicated, may hold values from 0 to 1023
Outputs:
- facet_strips: float32 [2, 2, 16, 256, 16384], P(None, None, 'fac', 'sub')
The draws below stay inside these ranges and needn't reach their ends.
Inputs may be any that keep to these rules, and one draw needn't show every extreme that they name: `sub_offsets`: column in the first entry (0 to 1), position in the second; within a column no position repeats. `coverage`: among the 8 slots of one index of sub at least one and at most 4 are present; on some index exactly 4.
All inputs are finite; a program needn't handle non-finite values.
Results may differ from the reference program's by a relative error of at most 0.0045.
Values may be sent and summed in bfloat16 or wider, within the bound.
No kernel may reach another device: no remote copies, remote signals or barrier semaphores. Data moves between devices by JAX's collectives and lax.ppermute only.
A program may use at most 256 MiB of HBM per device.

```python
import math
import jax
import jax.numpy as jnp
from jax import lax

XA = 512
XMYN = 256
VGRID = 128
FROWS = 4
COLS = 2
SLOT_DEV = 8
XM = 1024
YN = 16384
FACETS = 16
MOST = 4
SLOTS = 64


def subgrid_layout(key):
    owners = SLOTS // SLOT_DEV
    places = jax.random.permutation(jax.random.fold_in(key, 101), COLS * VGRID)[:SLOTS].astype(jnp.int32)
    column = places // VGRID
    position = places % VGRID
    counts = jax.random.randint(jax.random.fold_in(key, 102), (owners,), 1, MOST + 1)
    busiest = jax.random.randint(jax.random.fold_in(key, 103), (), 0, owners)
    counts = jnp.where(jnp.arange(owners) == busiest, MOST, counts)
    distance = jnp.abs(2 * position - (VGRID - 1))
    ranking = (distance * SLOTS + jnp.arange(SLOTS, dtype=jnp.int32)).reshape(owners, SLOT_DEV)
    placing = jnp.argsort(jnp.argsort(ranking, axis=1), axis=1)
    present = (placing < counts[:, None]).reshape(-1).astype(jnp.int32)
    return (column, position, present)


def draw_sub_offsets(key, part):
    column, position, present = subgrid_layout(key)
    return jnp.stack([column, position], axis=1).astype(jnp.int32)


def draw_coverage(key, part):
    column, position, present = subgrid_layout(key)
    return present


def set_ends(array, key, low, top_value):
    longest = array.shape.index(max(array.shape))
    spots = []
    for shift in (0, 1):
        where = [jax.random.randint(jax.random.fold_in(key, axis), (), 0, length) for axis, length in enumerate(array.shape)]
        where[longest] = (where[longest] + shift) % array.shape[longest]
        spots.append(tuple(where))
    return array.at[spots[0]].set(low).at[spots[1]].set(top_value)


def steps_of(own_key, extent, pieces, least, top_value):
    def one(axis_at, shards_of):
        steps = jax.random.uniform(jax.random.fold_in(jax.random.fold_in(own_key, 6), axis_at), (shards_of,), jnp.float32, least / len(pieces), top_value / len(pieces))
        return jnp.repeat(jnp.exp(steps), extent[axis_at] // shards_of).reshape((-1,) + (1,) * (len(extent) - axis_at - 1))

    gain = one(*pieces[0])
    for cut in pieces[1:]:
        gain = gain * one(*cut)
    return gain


def gaussian(stream_key, dims, width, reach, shards=(), kind=jnp.bfloat16):
    drawn = jax.random.normal(stream_key, dims, jnp.float32) * width
    if len(shards) > 0:
        drawn = steps_of(stream_key, dims, shards, -0.22, 0.18) * drawn
    return jnp.clip(drawn, min=-reach, max=reach).astype(kind)


def setup_inputs(seed: int = 0) -> dict:
    keys = jax.random.split(jax.random.key(seed), 5)
    subgrids = gaussian(keys[0], (2, SLOTS, XA, XA), 1.0, 6.0, ((1, 8), (2, 4)))
    sub_offsets = draw_sub_offsets(jax.random.fold_in(keys[4], 71), 0)
    coverage = draw_coverage(jax.random.fold_in(keys[4], 71), 0)
    facet_offsets = set_ends(jax.random.randint(keys[3], (2, FROWS), 0, XM), jax.random.fold_in(keys[3], 1), 0, XM - 1).astype(jnp.int32)
    return dict(subgrids=subgrids, sub_offsets=sub_offsets, coverage=coverage, facet_offsets=facet_offsets)


TAPER = 0.6

def build_tables(centres):
    middle = XMYN // 2
    samples = jnp.arange(XMYN, dtype=jnp.int32)
    pixels = jnp.arange(XA, dtype=jnp.int32)
    folded = jnp.mod((samples[:, None] - middle) * (samples[None, :] - middle), XMYN)
    kernel_angles = 2.0 * math.pi / XMYN * folded.astype(jnp.float32)
    kernel_real = jnp.cos(kernel_angles)
    kernel_imag = -jnp.sin(kernel_angles)
    taper = jnp.exp(-0.5 * ((samples.astype(jnp.float32) - middle) / (TAPER * middle)) ** 2)
    exact = lax.Precision.HIGHEST
    factor = 1.0 / math.sqrt(XMYN * XA)

    def one_table(centre):
        phases = jnp.mod((centre + samples[:, None] - middle) * (pixels[None, :] - XA // 2), XM)
        wave_angles = 2.0 * math.pi / XM * phases.astype(jnp.float32)
        wave_real = taper[:, None] * jnp.cos(wave_angles)
        wave_imag = taper[:, None] * jnp.sin(wave_angles)
        table_real = jnp.dot(kernel_real, wave_real, precision=exact, preferred_element_type=jnp.float32) - jnp.dot(kernel_imag, wave_imag, precision=exact, preferred_element_type=jnp.float32)
        table_imag = jnp.dot(kernel_real, wave_imag, precision=exact, preferred_element_type=jnp.float32) + jnp.dot(kernel_imag, wave_real, precision=exact, preferred_element_type=jnp.float32)
        return (jnp.stack([table_real, table_imag]) * factor).astype(jnp.bfloat16)
    return lax.map(one_table, centres)

def reference(subgrids, sub_offsets, coverage, facet_offsets):
    row_tables = build_tables(facet_offsets[0]).astype(jnp.float32)
    col_tables = build_tables(facet_offsets[1]).astype(jnp.float32)
    block_width = XMYN // 2
    strips = jnp.zeros((2, COLS, FACETS, XMYN, YN), jnp.float32)

    def one_slot(slot_index, strips):
        subgrid = subgrids[:, slot_index].astype(jnp.float32)
        real_u = jnp.einsum('fjx,xy->fjy', row_tables[:, 0], subgrid[0]) - jnp.einsum('fjx,xy->fjy', row_tables[:, 1], subgrid[1])
        imag_u = jnp.einsum('fjx,xy->fjy', row_tables[:, 0], subgrid[1]) + jnp.einsum('fjx,xy->fjy', row_tables[:, 1], subgrid[0])
        halfway = jnp.stack([real_u, imag_u]).astype(jnp.bfloat16)
        halfway = lax.optimization_barrier(halfway).astype(jnp.float32)
        real_v = jnp.einsum('ujy,vky->uvjk', halfway[0], col_tables[:, 0]) - jnp.einsum('ujy,vky->uvjk', halfway[1], col_tables[:, 1])
        imag_v = jnp.einsum('ujy,vky->uvjk', halfway[0], col_tables[:, 1]) + jnp.einsum('ujy,vky->uvjk', halfway[1], col_tables[:, 0])
        weight = coverage[slot_index].astype(jnp.float32)
        contrib = jnp.stack([real_v, imag_v]).reshape(2, FACETS, XMYN, XMYN) * weight
        column = sub_offsets[slot_index, 0].astype(jnp.int32)
        position = sub_offsets[slot_index, 1].astype(jnp.int32)
        lower = (jnp.mod(position - 1, VGRID) * block_width).astype(jnp.int32)
        upper = (position * block_width).astype(jnp.int32)
        anchor = jnp.zeros((), jnp.int32)
        for offset, segment in ((lower, contrib[..., :block_width]), (upper, contrib[..., block_width:])):
            corner = (anchor, column, anchor, anchor, offset)
            region = lax.dynamic_slice(strips, corner, (2, 1, FACETS, XMYN, block_width))
            strips = lax.dynamic_update_slice(strips, region + segment[:, None], corner)
        return strips
    return lax.fori_loop(0, SLOTS, one_slot, strips)
```

```python
import functools
import math

import jax
import jax.numpy as jnp
from jax import lax
from jax.experimental import pallas as pl
from jax.experimental.pallas import tpu as pltpu
from jax.sharding import PartitionSpec as P

XA = 512
XMYN = 256
VGRID = 128
FROWS = 4
COLS = 2
XM = 1024
YN = 16384
MOST = 4

TAPER = 0.6
HALF = XMYN // 2
LANES = 128


GROUPS = ((0, 1, 2), (3,))


def inner(z):
    return jnp.logical_and(z > 0, z < FROWS - 1)


def outer_of(z):
    return jnp.where(z < FROWS // 2, 0, FROWS - 1)


def tables_kernel(centres, table_u, table_v):
    f32 = jnp.float32
    z = lax.axis_index("fac")
    chosen = [centres[0, z], centres[0, outer_of(z)]] + [centres[1, v] for v in range(FROWS)]
    exact = functools.partial(jnp.dot, precision=lax.Precision.HIGHEST, preferred_element_type=f32)
    turns = XM // LANES
    m = lax.broadcasted_iota(jnp.int32, (turns, XMYN), 1) - HALF
    a = lax.broadcasted_iota(jnp.int32, (turns, XMYN), 0)
    taper = jnp.exp(-0.5 * (m.astype(f32) / (TAPER * HALF)) ** 2)
    coarse = 2.0 * math.pi / turns * jnp.bitwise_and(m * a, turns - 1).astype(f32)
    left_re, left_im = taper * jnp.cos(coarse), taper * jnp.sin(coarse)
    m = lax.broadcasted_iota(jnp.int32, (XMYN, LANES), 0) - HALF
    b = lax.broadcasted_iota(jnp.int32, (XMYN, LANES), 1)
    fine = 2.0 * math.pi / XM * jnp.bitwise_and(m * b, XM - 1).astype(f32)
    right_re, right_im = jnp.cos(fine), jnp.sin(fine)
    factor = 1.0 / math.sqrt(XMYN * XA)
    line_re = (exact(left_re, right_re) - exact(left_im, right_im)) * factor
    line_im = (exact(left_re, right_im) + exact(left_im, right_re)) * factor

    def spread(line):
        row = jnp.concatenate([line[i : i + 1] for i in range(turns)], axis=1)
        full = jnp.broadcast_to(row, (XMYN, XM))
        return pltpu.roll(full, XM - XA // 2, 1, stride=XM // XMYN, stride_axis=0)[:, :XA]

    base_re, base_im = spread(line_re), spread(line_im)
    x = lax.broadcasted_iota(jnp.int32, (8, XA), 1) - XA // 2
    row = lax.broadcasted_iota(jnp.int32, (8, XA), 0)
    centre = jnp.zeros((8, XA), jnp.int32)
    for t, value in enumerate(chosen):
        centre = jnp.where(row == t, value, centre)
    angle = 2.0 * math.pi / XM * jnp.bitwise_and(centre * x, XM - 1).astype(f32)
    phase_re, phase_im = jnp.cos(angle), jnp.sin(angle)
    for t in range(2):
        p_re, p_im = phase_re[t : t + 1], phase_im[t : t + 1]
        t_re = (base_re * p_re - base_im * p_im).astype(jnp.bfloat16)
        t_im = (base_re * p_im + base_im * p_re).astype(jnp.bfloat16)
        table_u[t, :XMYN, :XA] = t_re
        table_u[t, :XMYN, XA:] = -t_im
        table_u[t, XMYN:, :XA] = t_im
        table_u[t, XMYN:, XA:] = t_re
    turned_re, turned_im = jnp.transpose(base_re), jnp.transpose(base_im)
    down_re, down_im = jnp.transpose(phase_re), jnp.transpose(phase_im)
    for v in range(FROWS):
        p_re, p_im = down_re[:, 2 + v : 3 + v], down_im[:, 2 + v : 3 + v]
        t_re = (turned_re * p_re - turned_im * p_im).astype(jnp.bfloat16)
        t_im = (turned_re * p_im + turned_im * p_re).astype(jnp.bfloat16)
        table_v[v, 0, :XA, :] = t_re
        table_v[v, 0, XA:, :] = -t_im
        table_v[v, 1, :XA, :] = t_im
        table_v[v, 1, XA:, :] = t_re


def make_tables(facet_offsets):
    vmem = pl.BlockSpec(memory_space=pltpu.VMEM)
    return pl.pallas_call(
        tables_kernel,
        name="tables",
        out_shape=(
            jax.ShapeDtypeStruct((2, 2 * XMYN, 2 * XA), jnp.bfloat16),
            jax.ShapeDtypeStruct((FROWS, 2, 2 * XA, XMYN), jnp.bfloat16),
        ),
        in_specs=[pl.BlockSpec(memory_space=pltpu.SMEM)],
        out_specs=(vmem, vmem),
        cost_estimate=pl.CostEstimate(flops=10**9, bytes_accessed=8 * 2**20, transcendentals=10**5),
    )(facet_offsets)


def rows_kernel(table_u, own, near, across, far, mine, other, whole):
    z = lax.axis_index("fac")
    rows = own.shape[1]

    @pl.when(inner(z))
    def _():
        low = z < FROWS // 2
        places = (z, outer_of(z), FROWS - 1 - z, jnp.where(low, FROWS - 1, 0))
        for block, place in zip((own, near, across, far), places):
            for part in range(2):
                start = pl.multiple_of(part * XA + place * rows, rows)
                whole[pl.ds(start, rows), :] = block[part]
        for t, out in enumerate((mine, other)):
            total = jnp.dot(table_u[t], whole[...], preferred_element_type=jnp.float32)
            total = total.astype(jnp.bfloat16)
            out[0] = total[:XMYN]
            out[1] = total[XMYN:]


def row_pass(table_u, own, near, across, far):
    vmem = pl.BlockSpec(memory_space=pltpu.VMEM)
    shape = jax.ShapeDtypeStruct((2, XMYN, XA), jnp.bfloat16)
    return pl.pallas_call(
        rows_kernel,
        name="rows",
        out_shape=(shape, shape),
        in_specs=[vmem] * 5,
        out_specs=(vmem, vmem),
        scratch_shapes=[pltpu.VMEM((2 * XA, XA), jnp.bfloat16)],
        cost_estimate=pl.CostEstimate(flops=2**30, bytes_accessed=4 * 2**20, transcendentals=0),
    )(table_u, own, near, across, far)


def zeros_kernel(out, blank, sems):
    blank[...] = jnp.zeros_like(blank)
    parts = [(i, j, k) for i in range(2) for j in range(COLS) for k in range(out.shape[2])]
    copies = [pltpu.make_async_copy(blank, out.at[p], sems.at[n]) for n, p in enumerate(parts)]
    for copy in copies:
        copy.start()
    for copy in copies:
        copy.wait()


def make_zeros(shape):
    return pl.pallas_call(
        zeros_kernel,
        name="zeros",
        out_shape=jax.ShapeDtypeStruct(shape, jnp.float32),
        out_specs=pl.BlockSpec(memory_space=pl.ANY),
        scratch_shapes=[
            pltpu.VMEM(shape[3:], jnp.float32),
            pltpu.SemaphoreType.DMA((2 * COLS * shape[2],)),
        ],
        cost_estimate=pl.CostEstimate(flops=0, bytes_accessed=4 * math.prod(shape), transcendentals=0),
    )()


def columns_kernel(groups, owners, slot_dev, coverage, offsets, table_v, *refs):
    pieces = refs[: len(groups) * owners]
    out, lines, sums, slot_at, place_of, column_of, sems = refs[len(groups) * owners + 1 :]
    me = lax.axis_index("sub")
    rows = pieces[0].shape[2]
    total = owners * MOST
    for g, group in enumerate(groups):
        for d in range(owners):
            piece = pieces[g * owners + d]
            for n, c in enumerate(group):
                start = (d * MOST + c) * rows
                for part in range(2):
                    lines[start : start + rows, part * XA : (part + 1) * XA] = piece[n, part]
    for v in range(FROWS):
        for part in range(2):
            product = jnp.dot(lines[...], table_v[v, part], preferred_element_type=jnp.float32)
            sums[:, part, v] = product.reshape(total, rows, XMYN)

    @pl.loop(0, COLS * VGRID)
    def _(n):
        slot_at[n] = -1

    @pl.loop(0, total)
    def _(t):
        place_of[t] = -1

    @pl.loop(0, owners)
    def _(d):
        source = jnp.bitwise_xor(me, d)

        def scan(i, count):
            slot = source * slot_dev + i
            present = jnp.logical_and(coverage[slot] > 0, count < MOST)

            @pl.when(present)
            def _():
                t = d * MOST + count
                column, place = offsets[slot, 0], offsets[slot, 1]
                slot_at[column * VGRID + place] = t
                place_of[t] = place
                column_of[t] = column

            return count + present.astype(jnp.int32)

        lax.fori_loop(0, slot_dev, scan, jnp.int32(0))

    def copies(t):
        place, column = place_of[t], column_of[t]
        before = lax.rem(place + VGRID - 1, VGRID)

        def to(block, low, sem):
            where = pl.ds(pl.multiple_of(block * HALF, HALF), HALF)
            return pltpu.make_async_copy(
                sums.at[t, :, :, :, pl.ds(low, HALF)],
                out.at[:, column, :, :, where],
                sems.at[t, sem],
            )

        return slot_at[column * VGRID + before] < 0, to(before, 0, 0), to(place, HALF, 1)

    @pl.loop(0, total)
    def _(t):
        @pl.when(place_of[t] >= 0)
        def _():
            after = lax.rem(place_of[t] + 1, VGRID)
            right = slot_at[column_of[t] * VGRID + after]

            @pl.when(right >= 0)
            def _():
                sums[t, :, :, :, HALF:] += sums[right, :, :, :, :HALF]

    @pl.loop(0, total)
    def _(t):
        @pl.when(place_of[t] >= 0)
        def _():
            alone, lower, upper = copies(t)
            upper.start()

            @pl.when(alone)
            def _():
                lower.start()

    @pl.loop(0, total)
    def _(t):
        @pl.when(place_of[t] >= 0)
        def _():
            alone, lower, upper = copies(t)
            upper.wait()

            @pl.when(alone)
            def _():
                lower.wait()


def column_pass(groups, owners, slot_dev, coverage, offsets, table_v, pieces, blank):
    vmem = pl.BlockSpec(memory_space=pltpu.VMEM)
    smem = pl.BlockSpec(memory_space=pltpu.SMEM)
    rows = pieces[0].shape[2]
    total = owners * MOST
    return pl.pallas_call(
        functools.partial(columns_kernel, groups, owners, slot_dev),
        name="columns",
        out_shape=jax.ShapeDtypeStruct(blank.shape, blank.dtype),
        in_specs=[smem, smem, vmem] + [vmem] * len(pieces) + [pl.BlockSpec(memory_space=pl.ANY)],
        out_specs=pl.BlockSpec(memory_space=pl.ANY),
        scratch_shapes=[
            pltpu.VMEM((total * rows, 2 * XA), jnp.bfloat16),
            pltpu.VMEM((total, 2, FROWS, rows, XMYN), jnp.float32),
            pltpu.SMEM((COLS * VGRID,), jnp.int32),
            pltpu.SMEM((total,), jnp.int32),
            pltpu.SMEM((total,), jnp.int32),
            pltpu.SemaphoreType.DMA((total, 2)),
        ],
        input_output_aliases={3 + len(pieces): 0},
        cost_estimate=pl.CostEstimate(flops=4 * 2**30, bytes_accessed=14 * 2**20, transcendentals=0),
    )(coverage, offsets, table_v, *pieces, blank)


def present_slots(coverage, owners, slot_dev):
    first = lax.axis_index("sub") * slot_dev
    mask = lax.dynamic_slice_in_dim(coverage, first, slot_dev) > 0
    n = jnp.arange(slot_dev, dtype=jnp.int32)
    rank = jnp.sum(jnp.where(mask[None, :] & (n[None, :] < n[:, None]), 1, 0), axis=1)
    chosen = mask[None, :] & (rank[None, :] == jnp.arange(MOST, dtype=jnp.int32)[:, None])
    return jnp.sum(jnp.where(chosen, n[None, :], 0), axis=1)


def packed(subgrids, sub_offsets, coverage, facet_offsets):
    owners = lax.axis_size("sub")
    slot_dev = subgrids.shape[1]
    z = lax.axis_index("fac")
    me = lax.axis_index("sub")
    index = present_slots(coverage, owners, slot_dev)
    raws = [
        lax.dynamic_index_in_dim(subgrids, index[c], 1, keepdims=False) for c in range(MOST)
    ]
    last = FROWS - 1
    out_pairs = [(0, 1), (last, last - 1)]
    across_pairs = [(1, 2), (2, 1)]
    far_pairs = [(0, 2), (last, 1)]
    back_pairs = [(1, 0), (last - 1, last)]
    table_u, table_v = make_tables(facet_offsets)
    rows = XMYN // owners
    halves = []
    for c in range(MOST):
        near = lax.ppermute(raws[c], "fac", out_pairs)
        across = lax.ppermute(raws[c], "fac", across_pairs)
        far = lax.ppermute(raws[c], "fac", far_pairs)
        mine, other = row_pass(table_u, raws[c], near, across, far)
        back = lax.ppermute(other, "fac", back_pairs)
        halves.append(jnp.where(inner(z), mine, back))
    blank = make_zeros((2, COLS, FROWS, rows, YN))
    pieces = []
    for group in GROUPS:
        for d in range(owners):
            start = jnp.bitwise_xor(me, d) * rows
            part = jnp.stack([lax.dynamic_slice_in_dim(halves[c], start, rows, 1) for c in group])
            if d > 0:
                part = lax.ppermute(part, "sub", [(i, i ^ d) for i in range(owners)])
            pieces.append(part)
    return column_pass(GROUPS, owners, slot_dev, coverage, sub_offsets, table_v, pieces, blank)


def build_tables(centres):
    middle = XMYN // 2
    samples = jnp.arange(XMYN, dtype=jnp.int32)
    pixels = jnp.arange(XA, dtype=jnp.int32)
    folded = jnp.mod((samples[:, None] - middle) * (samples[None, :] - middle), XMYN)
    kernel_angles = 2.0 * math.pi / XMYN * folded.astype(jnp.float32)
    kernel_real = jnp.cos(kernel_angles)
    kernel_imag = -jnp.sin(kernel_angles)
    taper = jnp.exp(-0.5 * ((samples.astype(jnp.float32) - middle) / (TAPER * middle)) ** 2)
    exact = lax.Precision.HIGHEST
    factor = 1.0 / math.sqrt(XMYN * XA)

    def one_table(centre):
        phases = jnp.mod((centre + samples[:, None] - middle) * (pixels[None, :] - XA // 2), XM)
        wave_angles = 2.0 * math.pi / XM * phases.astype(jnp.float32)
        wave_real = taper[:, None] * jnp.cos(wave_angles)
        wave_imag = taper[:, None] * jnp.sin(wave_angles)
        table_real = jnp.dot(
            kernel_real, wave_real, precision=exact, preferred_element_type=jnp.float32
        ) - jnp.dot(kernel_imag, wave_imag, precision=exact, preferred_element_type=jnp.float32)
        table_imag = jnp.dot(
            kernel_real, wave_imag, precision=exact, preferred_element_type=jnp.float32
        ) + jnp.dot(kernel_imag, wave_real, precision=exact, preferred_element_type=jnp.float32)
        return (jnp.stack([table_real, table_imag]) * factor).astype(jnp.bfloat16)

    return lax.map(one_table, centres)


def dense_columns(halfway, table_v):
    real_v = jnp.einsum(
        "tjy,gky->gjtk", halfway[0], table_v[:, 0], preferred_element_type=jnp.float32
    ) - jnp.einsum("tjy,gky->gjtk", halfway[1], table_v[:, 1], preferred_element_type=jnp.float32)
    imag_v = jnp.einsum(
        "tjy,gky->gjtk", halfway[0], table_v[:, 1], preferred_element_type=jnp.float32
    ) + jnp.einsum("tjy,gky->gjtk", halfway[1], table_v[:, 0], preferred_element_type=jnp.float32)
    return jnp.stack([real_v, imag_v])


def general(subgrids, sub_offsets, coverage, facet_offsets):
    owners = lax.axis_size("sub")
    fac_count = lax.axis_size("fac")
    fac_dev = FROWS * FROWS // fac_count
    first = lax.axis_index("fac") * fac_dev
    row_centre = lax.dynamic_slice_in_dim(facet_offsets[0], first // FROWS, 1)
    col_centres = lax.dynamic_slice_in_dim(facet_offsets[1], first % FROWS, fac_dev)
    table_u = build_tables(row_centre)[0]
    table_v = build_tables(col_centres)
    slot_dev = subgrids.shape[1]
    orders = jnp.broadcast_to(jnp.arange(slot_dev, dtype=jnp.int32)[None, :], (owners, slot_dev))
    segment = lax.all_gather(subgrids, "fac", axis=2, tiled=True)
    real_u = jnp.einsum(
        "jx,txy->tjy", table_u[0], segment[0], preferred_element_type=jnp.float32
    ) - jnp.einsum("jx,txy->tjy", table_u[1], segment[1], preferred_element_type=jnp.float32)
    imag_u = jnp.einsum(
        "jx,txy->tjy", table_u[0], segment[1], preferred_element_type=jnp.float32
    ) + jnp.einsum("jx,txy->tjy", table_u[1], segment[0], preferred_element_type=jnp.float32)
    halfway = jnp.stack([real_u, imag_u]).astype(jnp.bfloat16)
    arrived = lax.all_to_all(halfway, "sub", split_axis=2, concat_axis=1, tiled=True)
    received = dense_columns(arrived, table_v)
    sources = (jnp.arange(owners, dtype=jnp.int32)[:, None] * slot_dev + orders).reshape(-1)
    total = sources.shape[0]
    source_mask = jnp.take(coverage, sources)
    source_column = jnp.take(sub_offsets[:, 0], sources)
    source_place = jnp.take(sub_offsets[:, 1], sources)
    target = jnp.where(source_mask > 0, source_column * VGRID + source_place, COLS * VGRID)
    inverse = (
        jnp.full((COLS * VGRID,), total, jnp.int32)
        .at[target]
        .set(jnp.arange(total, dtype=jnp.int32), mode="drop")
    )
    gathered = jnp.take(received, inverse, axis=3, mode="fill", fill_value=0.0)
    block_width = XMYN // 2
    rows_here = received.shape[2]
    gathered = gathered.reshape(2, fac_dev, rows_here, COLS, VGRID, XMYN)
    lower = jnp.roll(gathered[..., :block_width], -1, axis=4)
    upper = gathered[..., block_width:]
    strips = (lower + upper).reshape(2, fac_dev, rows_here, COLS, YN)
    return jnp.transpose(strips, (0, 3, 1, 2, 4))


def solution(mesh):
    owners, fac_count = mesh.shape["sub"], mesh.shape["fac"]
    fits = fac_count == FROWS and owners & (owners - 1) == 0 and XMYN // owners % 16 == 0
    placed = (P(None, "sub", "fac", None), P(), P(), P())
    return jax.shard_map(
        packed if fits else general,
        mesh=mesh,
        in_specs=placed,
        out_specs=P(None, None, "fac", "sub", None),
        check_vma=False,
    )
```
